32 devices in a mesh: grid: 8 (over y, x, core), sub: 4 (over z).
Axes of the slice: x: 2, y: 2, z: 4, core: 2. Of those that a mesh axis runs over, the one named last changes fastest.
Arguments:
- grid_x: bfloat16 [65536, 512], P(('grid', 'sub')), may hold values from -6 to 6
- mesh_h: bfloat16 [2048, 512], P(('grid', 'sub')), may hold values from -6 to 6
- gain_grid: float32 [512], replicated, may hold values from 0.1 to 1.9
- gain_mesh: float32 [512], replicated, may hold values from 0.1 to 1.9
- w_query: bfloat16 [512, 512], replicated, may hold values from -0.25 to 0.25
- w_key: bfloat16 [512, 512], replicated, may hold values from -0.25 to 0.25
- w_value: bfloat16 [512, 512], replicated, may hold values from -0.25 to 0.25
- w_out: bfloat16 [512, 512], replicated, may hold values from -0.25 to 0.25
- edge_bias: float32 [2048, 384], P(('grid', 'sub')), may hold values from -9 to 300
- neighbours: int32 [2048, 96], P(('grid', 'sub')), may hold values from 0 to 767, as said below
- valid: int32 [2048, 96], P(('grid', 'sub')), may hold values from 0 to 1, as said below
- send_rows: int32 [32, 3, 4, 64], P(('grid', 'sub')), may hold values from 0 to 2047, as said below
- out_grad: bfloat16 [2048, 512], P(('grid', 'sub')), may hold values from -24 to 24
Outputs:
- mesh_out: bfloat16 [2048, 512], P(('grid', 'sub'))
- mesh_grad: bfloat16 [2048, 512], P(('grid', 'sub'))
- grid_grad: bfloat16 [65536, 512], P(('grid', 'sub'))
- weight_grads: float32 [4, 512, 512], replicated
The draws below stay inside these ranges and needn't reach their ends.
Inputs may be any that keep to these rules, and one draw needn't show every extreme that they name: `send_rows`: for each source device, slab offset and destination sub index the 64 local rows are distinct; rows sent to the slab below (o = 0) lie in the lower half of the device's 2048 rows, rows sent to the slab above (o = 2) in the upper half. `neighbours`: a slot (o * 4 + s) * 64 + t names row t of what device s of slab g - o + 1 sends to the node's device; slots of slabs outside the grid are never named; the 96 entries of a node are distinct; some slots are named by no node. The first two edges of every node are valid.
All inputs are finite; a program needn't handle non-finite values.
Results may differ from the reference program's by a relative error of at most 0.009.
Values may be sent and summed in bfloat16 or wider, within the bound.
A program may use at most 128 MiB of HBM per device.

```python
import jax
import jax.numpy as jnp
from jax import lax

FEATURE_WIDTH = 512
HEADS = 4
GRID_NEIGHBOURS = 96
G_DEV = 2048
MESH_PER_SHARD = 64
RANKS = 32
CAP = 64
SLOTS = 768
HEAD_DIM = 128
GRID = 65536
MESH = 2048
N_GRID = 8
N_SUB = 4


def pair_counts(key):
    count_key = jax.random.fold_in(key, 11)
    lowest = max(2, CAP // 2)
    counts = jax.random.randint(count_key, (RANKS, 3, N_SUB), lowest, CAP + 1)
    rank_ids = jnp.arange(RANKS)[:, None, None]
    offsets = jnp.arange(3)[None, :, None]
    subs = jnp.arange(N_SUB)[None, None, :]
    slab = rank_ids // N_SUB
    own_sub = rank_ids % N_SUB
    counts = jnp.where((offsets == 1) & (subs == own_sub), CAP, counts)
    source_slab = slab - offsets + 1
    inside = (source_slab >= 0) & (source_slab < N_GRID)
    return jnp.where(inside, counts, 0)


def draw_send_rows(key, part):
    subkeys = jax.random.split(jax.random.fold_in(key, 23), RANKS * 3 * N_SUB)
    half_rows = jax.vmap(lambda subkey: jax.random.permutation(subkey, G_DEV // 2)[:CAP])(subkeys)
    full_rows = jax.vmap(lambda subkey: jax.random.permutation(jax.random.fold_in(subkey, 5), G_DEV)[:CAP])(subkeys)
    half_rows = half_rows.reshape(RANKS, 3, N_SUB, CAP)
    full_rows = full_rows.reshape(RANKS, 3, N_SUB, CAP)
    offsets = jnp.arange(3)[None, :, None, None]
    picked = jnp.where(offsets == 0, half_rows, jnp.where(offsets == 2, half_rows + G_DEV // 2, full_rows))
    return picked.astype(jnp.int32)


def draw_neighbours(key, part):
    counts = pair_counts(key)
    slot_iota = jnp.arange(SLOTS)
    offset_of = slot_iota // (N_SUB * CAP)
    sub_of = slot_iota // CAP % N_SUB
    within = slot_iota % CAP
    owner = jnp.arange(MESH) // MESH_PER_SHARD
    limit = counts[owner[:, None], offset_of[None, :], sub_of[None, :]]
    used = within[None, :] < limit
    top_value = (1 << 30) // SLOTS
    noise = jax.random.randint(jax.random.fold_in(key, 37), (MESH, SLOTS), 0, top_value)
    ranked = jnp.where(used, noise * SLOTS + slot_iota[None, :], -1)
    chosen = lax.top_k(ranked, GRID_NEIGHBOURS)[1]
    return chosen.astype(jnp.int32)


def draw_valid(key, part):
    levels = jax.random.randint(jax.random.fold_in(key, 41), (MESH, GRID_NEIGHBOURS), 0, 5)
    column = jnp.arange(GRID_NEIGHBOURS)[None, :]
    return jnp.where((levels > 0) | (column < 2), 1, 0).astype(jnp.int32)


def draw_edge_bias(key, part):
    normal_key = jax.random.fold_in(jax.random.fold_in(key, 53), 0)
    base = jax.random.normal(normal_key, (MESH, HEADS, GRID_NEIGHBOURS), jnp.float32)
    base = jnp.clip(base, -4.0, 4.0)
    return base.reshape(MESH, HEADS * GRID_NEIGHBOURS).astype(jnp.float32)


def steps_of(rng, dims, cuts, least, high):
    loudness = 1.0
    for axis_at, shards_of in cuts:
        draws = jax.random.uniform(jax.random.fold_in(jax.random.fold_in(rng, 6), axis_at), (shards_of,), jnp.float32, least / len(cuts), high / len(cuts))
        loudness = loudness * jnp.repeat(jnp.exp(draws), dims[axis_at] // shards_of).reshape((-1,) + (1,) * (len(dims) - 1 - axis_at))
    return loudness


def scatter_about(stream_key, extent, deviation, bound, cuts=(), kind=jnp.bfloat16):
    values = deviation * jax.random.normal(stream_key, extent, jnp.float32)
    if cuts:
        values = values * steps_of(stream_key, extent, cuts, -0.22, 0.18)
    return jnp.clip(values, -bound, bound).astype(kind)


def setup_inputs(seed: int = 0) -> dict:
    streams_of = jax.random.split(jax.random.key(seed), 14)
    return {
        "grid_x": scatter_about(streams_of[0], (GRID, FEATURE_WIDTH), 1.0, 6.0, ((0, 32),)),
        "mesh_h": scatter_about(streams_of[1], (MESH, FEATURE_WIDTH), 1.0, 6.0, ((0, 32),)),
        "gain_grid": jnp.clip(1.0 + 0.18 * jax.random.normal(streams_of[2], (FEATURE_WIDTH,), jnp.float32), 0.1, 1.9),
        "gain_mesh": jnp.clip(1.0 + 0.18 * jax.random.normal(streams_of[3], (FEATURE_WIDTH,), jnp.float32), 0.1, 1.9),
        "w_query": scatter_about(streams_of[4], (FEATURE_WIDTH, FEATURE_WIDTH), FEATURE_WIDTH ** -0.5, 0.25),
        "w_key": scatter_about(streams_of[5], (FEATURE_WIDTH, FEATURE_WIDTH), FEATURE_WIDTH ** -0.5, 0.25),
        "w_value": scatter_about(streams_of[6], (FEATURE_WIDTH, FEATURE_WIDTH), FEATURE_WIDTH ** -0.5, 0.25),
        "w_out": scatter_about(streams_of[7], (FEATURE_WIDTH, FEATURE_WIDTH), FEATURE_WIDTH ** -0.5, 0.25),
        "edge_bias": draw_edge_bias(jax.random.fold_in(streams_of[13], 71), 0),
        "neighbours": draw_neighbours(jax.random.fold_in(streams_of[13], 71), 0),
        "valid": draw_valid(jax.random.fold_in(streams_of[13], 71), 0),
        "send_rows": draw_send_rows(jax.random.fold_in(streams_of[13], 71), 0),
        "out_grad": scatter_about(streams_of[12], (MESH, FEATURE_WIDTH), 4.0, 24.0, ((0, 32),)),
    }


EPSILON = 1e-06
NEG_FILL = -1e+30

def normalize(values_in, gain_row):
    widened = values_in.astype(jnp.float32)
    factor = lax.rsqrt(lax.optimization_barrier(jnp.mean(widened * widened, axis=-1, keepdims=True)) + EPSILON)
    return (widened, factor, (widened * factor * gain_row).astype(jnp.bfloat16))

def normalize_back(widened, factor, gain_row, upstream):
    scaled = gain_row * upstream
    inner_mean = lax.optimization_barrier(jnp.mean(widened * scaled, axis=-1, keepdims=True))
    return factor * scaled - widened * factor ** 3 * inner_mean

def reference(grid_x, mesh_h, gain_grid, gain_mesh, w_query, w_key, w_value, w_out, edge_bias, neighbours, valid, send_rows, out_grad):
    logit_scale = HEAD_DIM ** (-0.5)
    grid_wide, grid_factor, grid_normed = normalize(grid_x, gain_grid)
    keys = jnp.dot(grid_normed, w_key, preferred_element_type=jnp.float32).astype(jnp.bfloat16)
    values = jnp.dot(grid_normed, w_value, preferred_element_type=jnp.float32).astype(jnp.bfloat16)
    mesh_wide, mesh_factor, mesh_normed = normalize(mesh_h, gain_mesh)
    queries = (jnp.dot(mesh_normed, w_query, preferred_element_type=jnp.float32) * logit_scale).astype(jnp.bfloat16)
    offsets = jnp.arange(3, dtype=jnp.int32)[:, None]
    subs = jnp.arange(N_SUB, dtype=jnp.int32)[None, :]

    def per_device(state_pair, rank_id):
        grid_acc, grad_acc = state_pair
        slab = (rank_id // N_SUB).astype(jnp.int32)
        own_sub = (rank_id % N_SUB).astype(jnp.int32)
        src_slab = jnp.clip(slab - offsets + 1, 0, N_GRID - 1).astype(jnp.int32)
        src_rank = (src_slab * N_SUB + subs).astype(jnp.int32)
        rows = send_rows[src_rank, jnp.broadcast_to(offsets, (3, N_SUB)), own_sub]
        point_ids = (src_rank[:, :, None] * G_DEV + rows).reshape(SLOTS).astype(jnp.int32)
        row_start = (rank_id * MESH_PER_SHARD).astype(jnp.int32)
        node_q = lax.dynamic_slice_in_dim(queries, row_start, MESH_PER_SHARD, 0)
        node_wide = lax.dynamic_slice_in_dim(mesh_wide, row_start, MESH_PER_SHARD, 0)
        node_factor = lax.dynamic_slice_in_dim(mesh_factor, row_start, MESH_PER_SHARD, 0)
        node_normed = lax.dynamic_slice_in_dim(mesh_normed, row_start, MESH_PER_SHARD, 0)
        node_grad = lax.dynamic_slice_in_dim(out_grad, row_start, MESH_PER_SHARD, 0)
        mesh_node_bias = lax.dynamic_slice_in_dim(edge_bias, row_start, MESH_PER_SHARD, 0).reshape(MESH_PER_SHARD, HEADS, GRID_NEIGHBOURS)
        node_nbr = lax.dynamic_slice_in_dim(neighbours, row_start, MESH_PER_SHARD, 0)
        node_valid = lax.dynamic_slice_in_dim(valid, row_start, MESH_PER_SHARD, 0)
        edge_points = point_ids[node_nbr]
        edge_key_rows = keys[edge_points].astype(jnp.float32).reshape(MESH_PER_SHARD, GRID_NEIGHBOURS, HEADS, HEAD_DIM)
        edge_value_rows = values[edge_points].astype(jnp.float32).reshape(MESH_PER_SHARD, GRID_NEIGHBOURS, HEADS, HEAD_DIM)
        query_head_rows = node_q.astype(jnp.float32).reshape(MESH_PER_SHARD, HEADS, HEAD_DIM)
        score_matrix = jnp.einsum('fog,flog->fol', query_head_rows, edge_key_rows) + mesh_node_bias
        live_mask = (node_valid == 1)[:, None, :]
        row_peak = lax.optimization_barrier(jnp.max(jnp.where(live_mask, score_matrix, NEG_FILL), axis=2, keepdims=True))
        exp_terms = jnp.exp(jnp.where(live_mask, score_matrix - row_peak, NEG_FILL))
        attn_probs = exp_terms / lax.optimization_barrier(jnp.sum(exp_terms, axis=2, keepdims=True))
        probabilities_batch = attn_probs.astype(jnp.bfloat16)
        attended_rows = jnp.einsum('bao,boai->bai', probabilities_batch.astype(jnp.float32), edge_value_rows).reshape(MESH_PER_SHARD, FEATURE_WIDTH).astype(jnp.bfloat16)
        out_rows = (node_wide + jnp.dot(attended_rows, w_out, preferred_element_type=jnp.float32)).astype(jnp.bfloat16)
        grad_wo = jnp.dot(attended_rows.T, node_grad, preferred_element_type=jnp.float32)
        att_grad = jnp.dot(node_grad, w_out.T, preferred_element_type=jnp.float32).astype(jnp.bfloat16)
        head_gradient = att_grad.astype(jnp.float32).reshape(MESH_PER_SHARD, HEADS, HEAD_DIM)
        probability_gradient = jnp.einsum('fog,flog->fol', head_gradient, edge_value_rows)
        score_gradient = (attn_probs * (probability_gradient - lax.optimization_barrier(jnp.sum(attn_probs * probability_gradient, axis=2, keepdims=True)))).astype(jnp.bfloat16)
        query_gradient = (jnp.einsum('bao,boai->bai', score_gradient.astype(jnp.float32), edge_key_rows) * logit_scale).reshape(MESH_PER_SHARD, FEATURE_WIDTH).astype(jnp.bfloat16)
        key_per_edge = jnp.einsum('iuw,iuy->iwuy', score_gradient.astype(jnp.float32), query_head_rows).reshape(MESH_PER_SHARD * GRID_NEIGHBOURS, FEATURE_WIDTH)
        value_per_edge = jnp.einsum('iuw,iuy->iwuy', probabilities_batch.astype(jnp.float32), head_gradient).reshape(MESH_PER_SHARD * GRID_NEIGHBOURS, FEATURE_WIDTH)
        slot_ids = node_nbr.reshape(MESH_PER_SHARD * GRID_NEIGHBOURS)
        key_part = jax.ops.segment_sum(key_per_edge, slot_ids, num_segments=SLOTS).astype(jnp.bfloat16)
        value_part = jax.ops.segment_sum(value_per_edge, slot_ids, num_segments=SLOTS).astype(jnp.bfloat16)
        sent_normed = grid_normed[point_ids]
        grad_wk = jnp.dot(sent_normed.T, key_part, preferred_element_type=jnp.float32)
        grad_wv = jnp.dot(sent_normed.T, value_part, preferred_element_type=jnp.float32)
        slot_back = jnp.dot(key_part, w_key.T, preferred_element_type=jnp.float32) + jnp.dot(value_part, w_value.T, preferred_element_type=jnp.float32)
        grid_acc = grid_acc.at[point_ids].add(slot_back)
        grad_wq = jnp.dot(node_normed.T, query_gradient, preferred_element_type=jnp.float32)
        normed_grad = jnp.dot(query_gradient, w_query.T, preferred_element_type=jnp.float32)
        grad_rows = (node_grad.astype(jnp.float32) + normalize_back(node_wide, node_factor, gain_mesh, normed_grad)).astype(jnp.bfloat16)
        grad_acc = grad_acc + jnp.stack([grad_wq, grad_wk, grad_wv, grad_wo])
        return ((grid_acc, grad_acc), (out_rows, grad_rows))
    initial = (jnp.zeros((GRID, FEATURE_WIDTH), jnp.float32), jnp.zeros((4, FEATURE_WIDTH, FEATURE_WIDTH), jnp.float32))
    (grid_acc, grad_acc), (out_rows, grad_rows) = lax.scan(per_device, initial, jnp.arange(RANKS, dtype=jnp.int32))
    grid_grad = normalize_back(grid_wide, grid_factor, gain_grid, grid_acc).astype(jnp.bfloat16)
    return (out_rows.reshape(MESH, FEATURE_WIDTH), grad_rows.reshape(MESH, FEATURE_WIDTH), grid_grad, grad_acc)
```

```python
import functools

import jax
import jax.numpy as jnp
from jax import lax
from jax.experimental import pallas as pl
from jax.sharding import PartitionSpec as P

EPSILON = 1e-06
NEG_FILL = -1e30


def from_behind(block, axis, distance):
    devices = range(lax.axis_size(axis))
    route = [(i - distance, i) for i in devices if i - distance in devices]
    return lax.ppermute(block, axis, route)


def normalize(values_in, gain_row):
    widened = values_in.astype(jnp.float32)
    factor = lax.rsqrt(jnp.mean(widened * widened, axis=-1, keepdims=True) + EPSILON)
    return (widened, factor, (widened * factor * gain_row).astype(jnp.bfloat16))


def normalize_back(widened, factor, gain_row, upstream):
    scaled = gain_row * upstream
    inner_mean = jnp.mean(widened * scaled, axis=-1, keepdims=True)
    return factor * scaled - widened * factor**3 * inner_mean


def spread_edges(nbr_ref, rows_ref, out_ref):
    slots = out_ref.shape[2]
    fanout = nbr_ref.shape[1]
    slot_ids = lax.broadcasted_iota(jnp.int32, (slots, fanout), 0)
    for node in range(nbr_ref.shape[0]):
        names = slot_ids == nbr_ref[pl.ds(node, 1), :]
        onehot = jnp.where(names, 1.0, 0.0).astype(jnp.bfloat16)
        spread = lax.dot_general(
            rows_ref[node], onehot, (((1,), (1,)), ((), ())), preferred_element_type=jnp.float32
        )
        out_ref[node] = (spread[16:24] + spread[8:16]) + spread[:8]


def attend(scale, q_ref, k_ref, v_ref, ag_ref, bias_ref, live_ref, att_ref, qg_ref, back_ref):
    queries, keys, values, att_grad = q_ref[...], k_ref[...], v_ref[...], ag_ref[...]
    nt = (((1,), (1,)), ((), ()))
    tn = (((0,), (0,)), ((), ()))

    def dot(a, b, dims):
        return lax.dot_general(a, b, dims, preferred_element_type=jnp.float32)

    live = live_ref[0] > 0.5
    scores = dot(queries, keys, nt) + bias_ref[0]
    peak = jnp.max(jnp.where(live, scores, NEG_FILL), axis=1, keepdims=True)
    terms = jnp.exp(jnp.where(live, scores - peak, NEG_FILL))
    probs = terms / jnp.sum(terms, axis=1, keepdims=True)
    probs_b = probs.astype(jnp.bfloat16)
    nn = (((1,), (0,)), ((), ()))
    att_ref[...] = dot(probs_b, values, nn).astype(jnp.bfloat16)
    prob_grads = dot(att_grad, values, nt)
    score_grads = (
        probs * (prob_grads - jnp.sum(probs * prob_grads, axis=1, keepdims=True))
    ).astype(jnp.bfloat16)
    qg_ref[...] = (dot(score_grads, keys, nn) * scale).astype(jnp.bfloat16)
    back_ref[0] = dot(score_grads, queries, tn).astype(jnp.bfloat16)
    back_ref[1] = dot(probs_b, att_grad, tn).astype(jnp.bfloat16)


def reduce_weights(local_grads):
    return lax.psum(local_grads, ("grid", "sub"))


def shards(
    grid_x,
    mesh_h,
    gain_grid,
    gain_mesh,
    w_query,
    w_key,
    w_value,
    w_out,
    edge_bias,
    neighbours,
    valid,
    send_rows,
    out_grad,
):
    point_count, model_width = grid_x.shape
    node_count = mesh_h.shape[0]
    sub_count = send_rows.shape[2]
    slots_per = send_rows.shape[3]
    block = sub_count * slots_per
    slot_count = 3 * block
    fanout = neighbours.shape[1]
    head_count = edge_bias.shape[1] // fanout
    head_width = model_width // head_count
    logit_scale = head_width ** (-0.5)
    w_pair = jnp.concatenate([w_key, w_value], axis=1)
    grid_wide, grid_factor, grid_normed = normalize(grid_x, gain_grid)
    flat_rows = send_rows[0].reshape(slot_count)
    send_match = flat_rows[:, None] == jnp.arange(point_count, dtype=jnp.int32)[None, :]
    send_onehot = send_match.astype(jnp.bfloat16)
    sent_normed = jnp.dot(send_onehot, grid_normed, preferred_element_type=jnp.float32).astype(
        jnp.bfloat16
    )
    packet = sent_normed.reshape(3, sub_count, slots_per, model_width)
    packet_width = packet.shape[3]
    mixed = lax.all_to_all(packet, "sub", split_axis=1, concat_axis=1, tiled=True).reshape(
        3, block, packet_width
    )
    pieces = []
    for offset in (0, 1, 2):
        piece = mixed[offset]
        if offset != 1:
            piece = from_behind(piece, "grid", offset - 1)
        pieces.append(piece)
    arrived = jnp.concatenate(pieces, axis=0)
    recv_pair = jnp.dot(arrived, w_pair, preferred_element_type=jnp.float32).astype(jnp.bfloat16)
    bias = edge_bias.reshape(node_count, head_count, fanout)
    high = lax.reduce_precision(bias, 8, 7)
    middle = lax.reduce_precision(bias - high, 8, 7)
    low = bias - high - middle
    live_row = (valid == 1).astype(jnp.float32)[:, None, :]
    filler = jnp.zeros((node_count, 8 - head_count, fanout), jnp.float32)
    live_fill = jnp.concatenate([live_row, filler[:, 1:]], axis=1)
    edge_rows = jnp.concatenate([high, live_fill, middle, filler, low, filler], axis=1)
    group = 16
    dense = pl.pallas_call(
        spread_edges,
        grid=(node_count // group,),
        in_specs=[
            pl.BlockSpec((group, fanout), lambda i: (i, 0)),
            pl.BlockSpec((group, 24, fanout), lambda i: (i, 0, 0)),
        ],
        out_specs=pl.BlockSpec((group, 8, slot_count), lambda i: (i, 0, 0)),
        out_shape=jax.ShapeDtypeStruct((node_count, 8, slot_count), jnp.float32),
        cost_estimate=pl.CostEstimate(
            flops=2 * node_count * 24 * fanout * slot_count,
            bytes_accessed=32 * node_count * slot_count,
            transcendentals=0,
        ),
    )(neighbours, edge_rows.astype(jnp.bfloat16))
    dense = jnp.transpose(dense, (1, 0, 2))
    mesh_wide, mesh_factor, mesh_normed = normalize(mesh_h, gain_mesh)
    queries = (
        jnp.dot(mesh_normed, w_query, preferred_element_type=jnp.float32) * logit_scale
    ).astype(jnp.bfloat16)
    att_grad = jnp.einsum("me,de->md", out_grad, w_out, preferred_element_type=jnp.float32).astype(
        jnp.bfloat16
    )
    by_head = pl.BlockSpec((node_count, head_width), lambda h: (0, h))
    attended_rows, query_gradient, back = pl.pallas_call(
        functools.partial(attend, logit_scale),
        grid=(head_count,),
        in_specs=[
            by_head,
            pl.BlockSpec((slot_count, head_width), lambda h: (0, h)),
            pl.BlockSpec((slot_count, head_width), lambda h: (0, head_count + h)),
            by_head,
            pl.BlockSpec((1, node_count, slot_count), lambda h: (h, 0, 0)),
            pl.BlockSpec((1, node_count, slot_count), lambda h: (head_count, 0, 0)),
        ],
        out_specs=[
            by_head,
            by_head,
            pl.BlockSpec((2, slot_count, head_width), lambda h: (0, 0, h)),
        ],
        out_shape=[
            jax.ShapeDtypeStruct((node_count, model_width), jnp.bfloat16),
            jax.ShapeDtypeStruct((node_count, model_width), jnp.bfloat16),
            jax.ShapeDtypeStruct((2, slot_count, model_width), jnp.bfloat16),
        ],
        cost_estimate=pl.CostEstimate(
            flops=12 * node_count * slot_count * model_width,
            bytes_accessed=8 * slot_count * model_width,
            transcendentals=node_count * head_count * slot_count,
        ),
    )(queries, recv_pair, recv_pair, att_grad, dense, dense)
    mesh_out = (
        mesh_wide + jnp.dot(attended_rows, w_out, preferred_element_type=jnp.float32)
    ).astype(jnp.bfloat16)
    grad_wo = jnp.einsum("md,me->de", attended_rows, out_grad, preferred_element_type=jnp.float32)
    grad_wk = jnp.einsum("sd,se->de", arrived, back[0], preferred_element_type=jnp.float32)
    grad_wv = jnp.einsum("sd,se->de", arrived, back[1], preferred_element_type=jnp.float32)
    grad_wq = jnp.einsum(
        "md,me->de", mesh_normed, query_gradient, preferred_element_type=jnp.float32
    )
    weight_grads = reduce_weights(jnp.stack([grad_wq, grad_wk, grad_wv, grad_wo]))
    back_packet = (
        jnp.concatenate([back[0], back[1]], axis=1)
        .reshape(3, block, 2 * model_width)
    )
    home_pieces = []
    for offset in (0, 1, 2):
        piece = back_packet[offset]
        if offset != 1:
            piece = from_behind(piece, "grid", 1 - offset)
        home_pieces.append(piece)
    home = jnp.stack(home_pieces)
    home = home.reshape(3, sub_count, slots_per, 2 * model_width)
    returned = lax.all_to_all(home, "sub", split_axis=1, concat_axis=1, tiled=True).reshape(
        slot_count, 2 * model_width
    )
    slot_back = jnp.einsum("se,de->sd", returned, w_pair, preferred_element_type=jnp.float32)
    normed_grad = jnp.einsum(
        "sp,sd->pd",
        send_onehot,
        slot_back.astype(jnp.bfloat16),
        preferred_element_type=jnp.float32,
    )
    grid_grad = normalize_back(grid_wide, grid_factor, gain_grid, normed_grad).astype(jnp.bfloat16)
    mesh_normed_grad = jnp.einsum(
        "me,de->md", query_gradient, w_query, preferred_element_type=jnp.float32
    )
    mesh_grad = (
        out_grad.astype(jnp.float32)
        + normalize_back(mesh_wide, mesh_factor, gain_mesh, mesh_normed_grad)
    ).astype(jnp.bfloat16)
    return (mesh_out, mesh_grad, grid_grad, weight_grads)


def solution(mesh):
    in_specs = (
        P(("grid", "sub"), None),
        P(("grid", "sub"), None),
        P(),
        P(),
        P(),
        P(),
        P(),
        P(),
        P(("grid", "sub"), None),
        P(("grid", "sub"), None),
        P(("grid", "sub"), None),
        P(("grid", "sub"), None, None, None),
        P(("grid", "sub"), None),
    )
    out_specs = (P(("grid", "sub"), None), P(("grid", "sub"), None), P(("grid", "sub"), None), P())
    return jax.shard_map(shards, mesh=mesh, in_specs=in_specs, out_specs=out_specs, check_vma=False)
```
